256 devices in a mesh: shard: 32 (over z, x), tensor: 4 (over y), section: 2 (over core).
Axes of the slice: x: 4, y: 4, z: 8, core: 2. Of those that a mesh axis runs over, the one named last changes fastest.
Arguments:
- grad_parts: bfloat16 [8, 32, 1024, 1024], P(('tensor', 'section'), None, 'shard')
- weights: bfloat16 [32, 1024, 1024], P(None, 'shard', ('tensor', 'section')), may hold values from -6 to 6
- adam_m: float32 [32, 1024, 1024], P(None, 'shard', ('tensor', 'section'))
- adam_v: float32 [32, 1024, 1024], P(None, 'shard', ('tensor', 'section')), may hold values from 0.01 to 1
- left_stat: float32 [96, 1024, 1024], P('shard', None, ('tensor', 'section')), may hold values from -18 to 18
- right_stat: float32 [96, 1024, 1024], P('shard', None, ('tensor', 'section')), may hold values from -18 to 18
- left_root: bfloat16 [32, 1024, 1024], P(None, 'shard', ('tensor', 'section')), as said below
- right_root: bfloat16 [32, 1024, 1024], P(None, 'shard', ('tensor', 'section')), as said below
- block_owner: int32 [32], replicated, may hold values from 0 to 31, as said below
- block_matrix: int32 [32], replicated, may hold values from 0 to 4, as said below
- factors: float32 [832, 2048], P('shard', ('tensor', 'section')), may hold values from -6 to 6
- factor_grad: bfloat16 [832, 2048], P('shard', ('tensor', 'section')), may hold values from -6 to 6
- factor_m: float32 [832, 2048], P('shard', ('tensor', 'section')), may hold values from -3 to 3
- factor_v: float32 [832, 2048], P('shard', ('tensor', 'section')), may hold values from 0.2 to 2
Outputs:
- new_weights: bfloat16 [32, 1024, 1024], P(None, 'shard')
- adam_m_new: float32 [32, 1024, 1024], P(None, 'shard', ('tensor', 'section'))
- adam_v_new: float32 [32, 1024, 1024], P(None, 'shard', ('tensor', 'section'))
- left_new: float32 [96, 1024, 1024], P('shard', None, ('tensor', 'section'))
- right_new: float32 [96, 1024, 1024], P('shard', None, ('tensor', 'section'))
- factors_new: float32 [832, 2048], P('shard', ('tensor', 'section'))
- factor_m_new: float32 [832, 2048], P('shard', ('tensor', 'section'))
- factor_v_new: float32 [832, 2048], P('shard', ('tensor', 'section'))
The draws below stay inside these ranges and needn't reach their ends.
Inputs may be any that keep to these rules, and one draw needn't show every extreme that they name: `block_owner`: no owner holds more than 3 blocks, and some owner holds exactly 3. `block_matrix`: matrices 0 to 3 hold 4 blocks each, all other blocks belong to matrix 4. `left_root`: every block is symmetric. `right_root`: every block is symmetric.
All inputs are finite; a program needn't handle non-finite values.
Results may differ from the reference program's by a relative error of at most 0.014.
Values may be sent and summed in bfloat16 or wider, within the bound.
A program may use at most 128 MiB of HBM per device.

```python
import math
import jax
import jax.numpy as jnp
from jax import lax

D = 2048
B = 1024
MATS = 5
QD = 4
NBLK = 32
PARTS_SIZE = 8
CAP = 3
SLOTS = 96
ROWS_F = 832
N_SHARD = 32


def log_spread(key, array_shape, high):
    uniform_draw = jax.random.uniform(key, array_shape, jnp.float32)
    return jnp.exp(uniform_draw * math.log(high))


def draw_grad_parts(key, part):
    subkeys = jax.random.split(jax.random.fold_in(key, 3), 6)
    array_shape = (PARTS_SIZE, NBLK, B, B)
    noise_draw = jnp.clip(jax.random.normal(subkeys[0], array_shape, jnp.float32), -6.0, 6.0)
    block_scale = log_spread(subkeys[3], (1, NBLK, 1, 1), 4.0)
    row_scale = log_spread(subkeys[4], (1, NBLK, B, 1), 10.0)
    col_scale = log_spread(subkeys[5], (1, NBLK, 1, B), 10.0)
    return (0.01 / math.sqrt(PARTS_SIZE) * noise_draw * block_scale * row_scale * col_scale).astype(jnp.bfloat16)


def draw_adam_m(key, part):
    subkeys = jax.random.split(jax.random.fold_in(key, 5), 3)
    array_shape = (NBLK, B, B)
    row_place = jnp.arange(B, dtype=jnp.float32).reshape(1, B, 1) / B
    noise_draw = jnp.clip(jax.random.normal(subkeys[0], array_shape, jnp.float32), -6.0, 6.0)
    rising = jnp.exp(math.log(3.0) * row_place)
    row_scale = log_spread(subkeys[1], (NBLK, B, 1), 10.0)
    col_scale = log_spread(subkeys[2], (NBLK, 1, B), 10.0)
    return 0.03 * noise_draw * rising * row_scale * col_scale


def symmetric_root(key):
    subkeys = jax.random.split(key, 2)
    array_shape = (NBLK, B, B)
    raw_draw = jnp.clip(jax.random.normal(subkeys[0], array_shape, jnp.float32), -6.0, 6.0)
    diagonal = jax.random.uniform(subkeys[1], (NBLK, B, 1), jnp.float32, 1.0, 2.0)
    off_diagonal = (raw_draw + jnp.swapaxes(raw_draw, 1, 2)) * (0.4 / math.sqrt(2.0 * B))
    row_ids = jnp.arange(B, dtype=jnp.int32)
    on_diagonal = (row_ids[:, None] == row_ids[None, :])[None, :, :]
    return jnp.where(on_diagonal, diagonal, off_diagonal)


def draw_left_root(key, part):
    return symmetric_root(jax.random.fold_in(key, 7)).astype(jnp.bfloat16)


def draw_right_root(key, part):
    return symmetric_root(jax.random.fold_in(key, 9)).astype(jnp.bfloat16)


def draw_block_owner(key, part):
    subkeys = jax.random.split(jax.random.fold_in(key, 11), 2)
    slot_total = N_SHARD * CAP
    scores = jax.random.permutation(subkeys[0], slot_total).astype(jnp.int32)
    chosen = jax.random.randint(subkeys[1], (), 0, N_SHARD).astype(jnp.int32)
    slot_ids = jnp.arange(slot_total, dtype=jnp.int32)
    scores = jnp.where(slot_ids // CAP == chosen, slot_ids - slot_total, scores)
    ranking = jnp.argsort(scores, stable=True).astype(jnp.int32)
    return (ranking[:NBLK] // CAP).astype(jnp.int32)


def draw_block_matrix(key, part):
    positions = jnp.arange(NBLK, dtype=jnp.int32)
    matrix_ids = jnp.where(positions < 4 * QD, positions // QD, 4).astype(jnp.int32)
    return jax.random.permutation(jax.random.fold_in(key, 13), matrix_ids).astype(jnp.int32)


def shard_levels(own_key, shape, cuts, smallest, high):
    def one(dim, blocks):
        heights = jax.random.uniform(jax.random.fold_in(jax.random.fold_in(own_key, 6), dim), (blocks,), jnp.float32, smallest / len(cuts), high / len(cuts))
        return jnp.repeat(jnp.exp(heights), shape[dim] // blocks).reshape((-1,) + (1,) * (len(shape) - dim - 1))

    factor_of = one(*cuts[0])
    for cut in cuts[1:]:
        factor_of = factor_of * one(*cut)
    return factor_of


def bell_draw(own_key, extent, width, limit, cuts=(), kind=jnp.bfloat16):
    factor_of = shard_levels(own_key, extent, cuts, -0.22, 0.18) if cuts else 1.0
    values = jax.random.normal(own_key, extent, jnp.float32) * width * factor_of
    return jnp.minimum(jnp.maximum(values, -limit), limit).astype(kind)


def setup_inputs(seed: int = 0) -> dict:
    arg_keys = jax.random.split(jax.random.key(seed), 15)
    grad_parts = draw_grad_parts(jax.random.fold_in(arg_keys[14], 71), 0)
    weights = bell_draw(arg_keys[1], (NBLK, B, B), 1.0, 6.0, ((1, 32), (2, 8)))
    adam_m = draw_adam_m(jax.random.fold_in(arg_keys[14], 71), 0)
    adam_v = jnp.clip(jnp.exp(math.log(1.0) - 4.6051702 * jax.random.uniform(arg_keys[3], (NBLK, B, B), jnp.float32) ** shard_levels(arg_keys[3], (NBLK, B, B), ((1, 32), (2, 8)), -0.2, 0.2)), 0.01, 1.0)
    left_stat = bell_draw(arg_keys[4], (SLOTS, B, B), 3.0, 18.0, ((0, 32), (2, 8)), jnp.float32)
    right_stat = bell_draw(arg_keys[5], (SLOTS, B, B), 3.0, 18.0, ((0, 32), (2, 8)), jnp.float32)
    left_root = draw_left_root(jax.random.fold_in(arg_keys[14], 71), 0)
    right_root = draw_right_root(jax.random.fold_in(arg_keys[14], 71), 0)
    block_owner = draw_block_owner(jax.random.fold_in(arg_keys[14], 71), 0)
    block_matrix = draw_block_matrix(jax.random.fold_in(arg_keys[14], 71), 0)
    factors = bell_draw(arg_keys[10], (ROWS_F, D), 1.0, 6.0, ((0, 32), (1, 8)), jnp.float32)
    factor_grad = bell_draw(arg_keys[11], (ROWS_F, D), 1.0, 6.0, ((0, 32), (1, 8)))
    factor_m = bell_draw(arg_keys[12], (ROWS_F, D), 0.5, 3.0, ((0, 32), (1, 8)), jnp.float32)
    factor_v = jnp.clip(jnp.exp(math.log(2.0) - 2.3025851 * jax.random.uniform(arg_keys[13], (ROWS_F, D), jnp.float32) ** shard_levels(arg_keys[13], (ROWS_F, D), ((0, 32), (1, 8)), -0.2, 0.2)), 0.2, 2.0)
    return dict(grad_parts=grad_parts, weights=weights, adam_m=adam_m, adam_v=adam_v, left_stat=left_stat, right_stat=right_stat, left_root=left_root, right_root=right_root, block_owner=block_owner, block_matrix=block_matrix, factors=factors, factor_grad=factor_grad, factor_m=factor_m, factor_v=factor_v)


BETA_ONE = 0.9
BETA_TWO = 0.95
BETA_STAT = 0.95
LEARNING = 0.1
DECAY_RATE = 0.1
EPSILON = 1e-08
FLOOR_RATE = 1e-06
CORRECT_ONE = 1.0 - 0.9 ** 10
CORRECT_TWO = 1.0 - 0.95 ** 10

def adam_direction(grad_float, moment, second):
    moment_new = BETA_ONE * moment + (1.0 - BETA_ONE) * grad_float
    second_new = BETA_TWO * second + (1.0 - BETA_TWO) * grad_float * grad_float
    direction = moment_new / CORRECT_ONE / (jnp.sqrt(second_new / CORRECT_TWO) + EPSILON)
    return (moment_new, second_new, direction)

def slot_numbers(block_owner, capacity):
    positions = jnp.arange(block_owner.shape[0], dtype=jnp.int32)
    earlier = (block_owner[:, None] == block_owner[None, :]) & (positions[None, :] < positions[:, None])
    return (block_owner * capacity + lax.optimization_barrier(jnp.sum(earlier.astype(jnp.int32), axis=1))).astype(jnp.int32)

def reference(grad_parts, weights, adam_m, adam_v, left_stat, right_stat, left_root, right_root, block_owner, block_matrix, factors, factor_grad, factor_m, factor_v):
    gradient = lax.optimization_barrier(jnp.sum(grad_parts.astype(jnp.float32), axis=0)).astype(jnp.bfloat16)
    gradient = lax.optimization_barrier(gradient)
    grad_float = gradient.astype(jnp.float32)
    adam_m_new, adam_v_new, direction = adam_direction(grad_float, adam_m, adam_v)
    onehot = (block_matrix[:, None] == jnp.arange(MATS, dtype=jnp.int32)[None, :]).astype(jnp.float32)
    adam_norm = lax.optimization_barrier(jnp.sum(lax.optimization_barrier(jnp.sum(direction * direction, axis=(1, 2)))[:, None] * onehot, axis=0))

    def per_block(operands):
        block_grad, block_left, block_right = operands
        gram_left = jnp.dot(block_grad, block_grad.T, preferred_element_type=jnp.float32)
        gram_right = jnp.dot(block_grad.T, block_grad, preferred_element_type=jnp.float32)
        mixed = jnp.dot(block_left, block_grad, preferred_element_type=jnp.float32).astype(jnp.bfloat16)
        precond = jnp.dot(mixed, block_right, preferred_element_type=jnp.float32)
        return (gram_left, gram_right, precond)
    gram_left, gram_right, precond = lax.map(per_block, (gradient, left_root, right_root))
    slot = slot_numbers(block_owner, CAP)
    left_new = (BETA_STAT * left_stat).at[slot].set(BETA_STAT * left_stat[slot] + (1.0 - BETA_STAT) * gram_left)
    right_new = (BETA_STAT * right_stat).at[slot].set(BETA_STAT * right_stat[slot] + (1.0 - BETA_STAT) * gram_right)
    shampoo_norm = lax.optimization_barrier(jnp.sum(lax.optimization_barrier(jnp.sum(precond * precond, axis=(1, 2)))[:, None] * onehot, axis=0))
    counts = lax.optimization_barrier(jnp.sum(onehot, axis=0)) * float(B * B)
    graft_scale = jnp.sqrt(adam_norm / (shampoo_norm + FLOOR_RATE * counts))
    block_scale = lax.optimization_barrier(jnp.sum(onehot * graft_scale[None, :], axis=1))
    precond_half = lax.optimization_barrier(precond.astype(jnp.bfloat16)).astype(jnp.float32)
    weights_float = weights.astype(jnp.float32)
    new_weights = (weights_float - LEARNING * (block_scale[:, None, None] * precond_half + DECAY_RATE * weights_float)).astype(jnp.bfloat16)
    factor_m_new, factor_v_new, factor_step = adam_direction(factor_grad.astype(jnp.float32), factor_m, factor_v)
    factors_new = factors - LEARNING * (factor_step + DECAY_RATE * factors)
    return (new_weights, adam_m_new, adam_v_new, left_new, right_new, factors_new, factor_m_new, factor_v_new)
```

```python
import jax
import jax.numpy as jnp
from jax import lax
from jax.sharding import PartitionSpec as P

B = 1024
MATS = 5


BETA_ONE = 0.9
BETA_TWO = 0.95
BETA_STAT = 0.95
LEARNING = 0.1
DECAY_RATE = 0.1
EPSILON = 1e-08
FLOOR_RATE = 1e-06
CORRECT_ONE = 1.0 - 0.9**10
CORRECT_TWO = 1.0 - 0.95**10


def adam_direction(grad_float, moment, second):
    moment_new = BETA_ONE * moment + (1.0 - BETA_ONE) * grad_float
    second_new = BETA_TWO * second + (1.0 - BETA_TWO) * grad_float * grad_float
    direction = moment_new / CORRECT_ONE / (jnp.sqrt(second_new / CORRECT_TWO) + EPSILON)
    return (moment_new, second_new, direction)


def slot_numbers(block_owner, capacity):
    positions = jnp.arange(block_owner.shape[0], dtype=jnp.int32)
    earlier = (block_owner[:, None] == block_owner[None, :]) & (
        positions[None, :] < positions[:, None]
    )
    return block_owner * capacity + jnp.sum(earlier.astype(jnp.int32), axis=1)


def slot_contents(slot, slot_total):
    positions = jnp.arange(slot.shape[0], dtype=jnp.int32)
    matches = jnp.arange(slot_total, dtype=jnp.int32)[:, None] == slot[None, :]
    occupied = jnp.any(matches, axis=1)
    block_ids = jnp.sum(jnp.where(matches, positions[None, :], 0), axis=1)
    return (block_ids, occupied)


def fill_slots(tiles, block_ids, occupied):
    picked = jnp.take(tiles, block_ids, axis=0)
    return jnp.where(occupied[:, None, None], picked, jnp.zeros_like(picked))


def shards(
    grad_parts,
    weights,
    adam_m,
    adam_v,
    left_stat,
    right_stat,
    left_root,
    right_root,
    block_owner,
    block_matrix,
    factors,
    factor_grad,
    factor_m,
    factor_v,
):
    capacity = left_stat.shape[0]
    owners = lax.axis_size("shard")
    owner_index = lax.axis_index("shard")
    group_index = lax.axis_index(("tensor", "section"))
    partials = grad_parts[0].astype(jnp.float32)
    gradient = lax.psum_scatter(
        partials.astype(jnp.bfloat16), ("tensor", "section"), scatter_dimension=2, tiled=True
    )
    gradient = lax.optimization_barrier(gradient)
    grad_float = gradient.astype(jnp.float32)
    adam_m_new, adam_v_new, direction = adam_direction(grad_float, adam_m, adam_v)
    matrix_range = jnp.arange(MATS, dtype=jnp.int32)
    onehot = (block_matrix[:, None] == matrix_range[None, :]).astype(jnp.float32)
    adam_part = jnp.sum(jnp.sum(direction * direction, axis=(1, 2))[:, None] * onehot, axis=0)
    slot = slot_numbers(block_owner, capacity)
    block_ids, occupied = slot_contents(slot, owners * capacity)
    slab_width = gradient.shape[2]
    def to_block(x):
        return lax.all_to_all(x, "shard", split_axis=0, concat_axis=1, tiled=True)

    left_cols = to_block(left_root)
    right_cols = to_block(right_root)
    left_full = lax.all_gather(left_cols, ("tensor", "section"), axis=2, tiled=True)
    grad_cols = to_block(gradient)
    mixed = jnp.einsum(
        "sij,sjc->sic", left_full, grad_cols, preferred_element_type=jnp.float32
    ).astype(jnp.bfloat16)
    mixed_full = lax.all_gather(mixed, ("tensor", "section"), axis=2, tiled=True)
    precond = jnp.einsum("sik,skc->sic", mixed_full, right_cols, preferred_element_type=jnp.float32)
    own_matrix = lax.dynamic_slice_in_dim(block_matrix, owner_index, 1)
    own_onehot = (own_matrix == matrix_range).astype(jnp.float32)
    shampoo_part = jnp.sum(precond * precond) * own_onehot
    precond_tile = lax.all_to_all(
        precond.astype(jnp.bfloat16), "shard", split_axis=1, concat_axis=0, tiled=True
    ).astype(jnp.float32)
    slot_cols = to_block(fill_slots(gradient, block_ids, occupied))
    grad_full = lax.all_gather(slot_cols, ("tensor", "section"), axis=2, tiled=True)
    first_row = group_index * slab_width
    grad_rows_own = lax.dynamic_slice_in_dim(grad_full, first_row, slab_width, 1)
    gram_left = jnp.einsum(
        "sik,sjk->sij", grad_full, grad_rows_own, preferred_element_type=jnp.float32
    )
    gram_right = jnp.einsum(
        "ski,skj->sij", grad_full, slot_cols, preferred_element_type=jnp.float32
    )
    left_new = BETA_STAT * left_stat + (1.0 - BETA_STAT) * gram_left
    right_new = BETA_STAT * right_stat + (1.0 - BETA_STAT) * gram_right
    adam_norm, shampoo_norm = lax.psum((adam_part, shampoo_part), ("shard", "tensor", "section"))
    counts = jnp.sum(onehot, axis=0) * float(B * B)
    graft_scale = jnp.sqrt(adam_norm / (shampoo_norm + FLOOR_RATE * counts))
    block_scale = jnp.sum(onehot * graft_scale[None, :], axis=1)
    weights_float = weights.astype(jnp.float32)
    updated = (
        weights_float
        - LEARNING * (block_scale[:, None, None] * precond_tile + DECAY_RATE * weights_float)
    ).astype(jnp.bfloat16)
    factor_m_new, factor_v_new, factor_step = adam_direction(
        factor_grad.astype(jnp.float32), factor_m, factor_v
    )
    factors_new = factors - LEARNING * (factor_step + DECAY_RATE * factors)
    new_weights = lax.all_gather(updated, ("tensor", "section"), axis=2, tiled=True)
    return (
        new_weights,
        adam_m_new,
        adam_v_new,
        left_new,
        right_new,
        factors_new,
        factor_m_new,
        factor_v_new,
    )


def solution(mesh):
    in_specs = (
        P(("tensor", "section"), None, "shard", None),
        P(None, "shard", ("tensor", "section")),
        P(None, "shard", ("tensor", "section")),
        P(None, "shard", ("tensor", "section")),
        P("shard", None, ("tensor", "section")),
        P("shard", None, ("tensor", "section")),
        P(None, "shard", ("tensor", "section")),
        P(None, "shard", ("tensor", "section")),
        P(),
        P(),
        P("shard", ("tensor", "section")),
        P("shard", ("tensor", "section")),
        P("shard", ("tensor", "section")),
        P("shard", ("tensor", "section")),
    )
    out_specs = (
        P(None, "shard", None),
        P(None, "shard", ("tensor", "section")),
        P(None, "shard", ("tensor", "section")),
        P("shard", None, ("tensor", "section")),
        P("shard", None, ("tensor", "section")),
        P("shard", ("tensor", "section")),
        P("shard", ("tensor", "section")),
        P("shard", ("tensor", "section")),
    )
    return jax.shard_map(shards, mesh=mesh, in_specs=in_specs, out_specs=out_specs, check_vma=False)
```

```python
import jax
import jax.numpy as jnp
from jax import lax
from jax.experimental import pallas as pl
from jax.experimental.pallas import tpu as pltpu
from jax.sharding import PartitionSpec as P

B = 1024
MATS = 5

BETA_ONE = 0.9
BETA_TWO = 0.95
BETA_STAT = 0.95
LEARNING = 0.1
DECAY_RATE = 0.1
EPSILON = 1e-08
FLOOR_RATE = 1e-06
CORRECT_ONE = 1.0 - 0.9**10
CORRECT_TWO = 1.0 - 0.95**10

MESH = pl.DeviceIdType.MESH
F32 = jnp.float32
BF16 = jnp.bfloat16
OWNERS = 32
RING = 4
GROUP = 8
ROWS = B // OWNERS
WIDTH = B // GROUP
HALF = B // 2
CAP = 3


def adam_direction(grad_float, moment, second):
    moment_new = BETA_ONE * moment + (1.0 - BETA_ONE) * grad_float
    second_new = BETA_TWO * second + (1.0 - BETA_TWO) * grad_float * grad_float
    direction = moment_new / CORRECT_ONE / (jnp.sqrt(second_new / CORRECT_TWO) + EPSILON)
    return (moment_new, second_new, direction)


def slot_numbers(block_owner, capacity):
    positions = jnp.arange(block_owner.shape[0], dtype=jnp.int32)
    earlier = (block_owner[:, None] == block_owner[None, :]) & (
        positions[None, :] < positions[:, None]
    )
    return block_owner * capacity + jnp.sum(earlier.astype(jnp.int32), axis=1)


def slot_contents(slot, slot_total):
    positions = jnp.arange(slot.shape[0], dtype=jnp.int32)
    matches = jnp.arange(slot_total, dtype=jnp.int32)[:, None] == slot[None, :]
    occupied = jnp.any(matches, axis=1)
    block_ids = jnp.sum(jnp.where(matches, positions[None, :], 0), axis=1)
    return (block_ids, occupied)


class Copy:
    def __init__(self, src, dst, send, recv, target, landing=None):
        self.out = pltpu.make_async_remote_copy(
            src_ref=src, dst_ref=dst, send_sem=send, recv_sem=recv, device_id=target,
            device_id_type=MESH,
        )
        here = dst if landing is None else landing
        self.into = pltpu.make_async_remote_copy(
            src_ref=here, dst_ref=here, send_sem=send, recv_sem=recv, device_id=target,
            device_id_type=MESH,
        )

    def start(self):
        self.out.start()

    def wait_recv(self):
        self.into.wait_recv()

    def wait_send(self):
        self.out.wait_send()


def span(start, size):
    return pl.ds(pl.multiple_of(start, size), size)


def kernel(
    ids_ref, parts, weights, adam_m, adam_v, left_stat, right_stat, left_root, right_root,
    mask, same, new_w, m_out, v_out, left_out, right_out,
    mine, pre, ps, rel_a, rel_b, from_minus, from_plus, grad, by_block, packed, left_full, mixed_full,
    new_full, slots, grad_cols, right_cols, pre_half, pre_tile, w_buf, m_buf, v_buf, ls_buf,
    rs_buf, tile_one, norm_one, tile_two, norm_two, sums, scales,
    send_sem, recv_sem, local_sem,
):
    s = lax.axis_index("shard")
    t = lax.axis_index("tensor")
    c = lax.axis_index("section")
    j = t * 2 + c
    up, down, across = lax.rem(t + 1, RING), lax.rem(t + 3, RING), lax.rem(t + 2, RING)
    to_up, to_down = {"tensor": up}, {"tensor": down}
    to_mate = {"section": 1 - c}
    own_cols = span(j * WIDTH, WIDTH)
    own_rows = span(s * ROWS, ROWS)
    counters = {"sem": 0, "local": 0}
    sent = []

    def new_sem():
        index = counters["sem"]
        counters["sem"] += 1
        return send_sem.at[index], recv_sem.at[index]

    def local(src, dst):
        index = counters["local"]
        counters["local"] += 1
        copy = pltpu.make_async_copy(src, dst, local_sem.at[index])
        copy.start()
        return copy

    def remote(src, dst, target, landing=None):
        send, recv = new_sem()
        copy = Copy(src, dst, send, recv, target, landing)
        sent.append(copy)
        return copy

    class Exchange:
        def __init__(self, src, dst, size, fixed=False):
            self.src, self.dst, self.size, self.fixed = src, dst, size, fixed
            self.send, self.recv = new_sem()
            whole = dst(pl.ds(0, (OWNERS - 1) * size))
            self.all = pltpu.make_async_remote_copy(
                src_ref=whole, dst_ref=whole, send_sem=self.send, recv_sem=self.recv,
                device_id={"shard": lax.rem(s + 1, OWNERS)}, device_id_type=MESH,
            )
            sent.append(self)

        def start(self):
            def one(k, carry):
                p = lax.rem(s + k, OWNERS)
                pltpu.make_async_remote_copy(
                    src_ref=self.src(p), dst_ref=self.dst(span(s * self.size, self.size)),
                    send_sem=self.send, recv_sem=self.recv, device_id={"shard": p},
                    device_id_type=MESH,
                ).start()
                return carry

            lax.fori_loop(1, OWNERS, one, 0)

        def wait_recv(self):
            self.all.wait_recv()

        def wait_send(self):
            self.all.wait_send()

    class Gather:
        def __init__(self, full):
            def part(slab, first, size):
                return full.at[pl.ds(first, size), span(slab * WIDTH, WIDTH)]

            own = j
            below, above, far = down * 2 + c, up * 2 + c, across * 2 + c
            lo, hi = (0, HALF), (HALF, HALF)
            self.up_lo = remote(part(own, *lo), part(own, *lo), to_up, part(below, *lo))
            self.up_hi = remote(part(own, *hi), part(own, *hi), to_up, part(below, *hi))
            self.down_hi = remote(part(own, *hi), part(own, *hi), to_down, part(above, *hi))
            self.down_lo = remote(part(own, *lo), part(own, *lo), to_down, part(above, *lo))
            self.fwd_up = remote(part(below, *lo), part(below, *lo), to_up, part(far, *lo))
            self.fwd_down = remote(part(above, *hi), part(above, *hi), to_down, part(far, *hi))
            mates = []
            for row in (t, down, up, across):
                mates.append(
                    remote(
                        part(row * 2 + c, 0, B), part(row * 2 + c, 0, B), to_mate,
                        part(row * 2 + 1 - c, 0, B),
                    )
                )
            self.mates = mates

        def start(self):
            self.up_lo.start()
            self.down_hi.start()
            self.up_hi.start()
            self.down_lo.start()
            self.mates[0].start()

        def relay_one(self):
            self.up_lo.wait_recv()
            self.fwd_up.start()
            self.down_hi.wait_recv()
            self.fwd_down.start()

        def relay_two(self):
            self.up_hi.wait_recv()
            self.mates[1].start()
            self.down_lo.wait_recv()
            self.mates[2].start()

        def relay_three(self):
            self.fwd_up.wait_recv()
            self.fwd_down.wait_recv()
            self.mates[3].start()

        def finish(self):
            for mate in self.mates:
                mate.wait_recv()

    with jax.named_scope("entry"):
        barrier = pltpu.get_barrier_semaphore()

        def greet(k, carry):
            pl.semaphore_signal(
                barrier, inc=1, device_id={"shard": lax.rem(s + k, OWNERS)}, device_id_type=MESH
            )
            return carry

        lax.fori_loop(1, OWNERS, greet, 0)

        def greet_row(q, carry):
            other = lax.rem(j + q, GROUP)
            pl.semaphore_signal(
                barrier, inc=1, device_id={"tensor": other // 2, "section": lax.rem(other, 2)},
                device_id_type=MESH,
            )
            return carry

        lax.fori_loop(1, GROUP, greet_row, 0)

        order = (across, up, down, t)
        mine_in = []
        for slot, row in enumerate(order):
            mine_in.append(
                local(parts.at[:, span((row * 2 + c) * WIDTH, WIDTH)], mine.at[slot])
            )
        right_own = local(right_root.at[own_rows, :], right_cols.at[own_rows, :])
        left_own = local(left_root.at[own_rows, :], left_full.at[own_rows, own_cols])
        m_in = local(adam_m, m_buf)
        v_in = local(adam_v, v_buf)
        w_in = local(weights, w_buf)
        ls_in = local(left_stat, ls_buf)
        rs_in = local(right_stat, rs_buf)
        pl.semaphore_wait(barrier, OWNERS - 1 + GROUP - 1)

    with jax.named_scope("reduce"):
        pairs = []
        for slot, row in enumerate(order):
            pairs.append(
                remote(
                    parts.at[:, span((row * 2 + 1 - c) * WIDTH, WIDTH)], pre.at[slot], to_mate
                )
            )
        for pair in pairs:
            pair.start()
        left_move = Exchange(
            lambda p: left_root.at[span(p * ROWS, ROWS), :],
            lambda rows: left_full.at[rows, own_cols], ROWS,
        )
        right_move = Exchange(
            lambda p: right_root.at[span(p * ROWS, ROWS), :],
            lambda rows: right_cols.at[rows, :], ROWS,
        )
        left_move.start()
        right_move.start()

        lo, hi = pl.ds(0, HALF), pl.ds(HALF, HALF)
        chunk = 64

        def add_up(target, first, rows, terms):
            def one(i, carry):
                at = span(first + i * chunk, chunk)
                total = terms[0](at).astype(F32)
                for term in terms[1:]:
                    total = total + term(at).astype(F32)
                target[at, :] = total.astype(BF16)
                return carry

            lax.fori_loop(0, rows // chunk, one, 0)

        def both(slot):
            mine_in[slot].wait()
            pairs[slot].wait_recv()
            return (lambda at: mine[slot, at, :], lambda at: pre[slot, at, :])

        far_up = remote(ps.at[0, lo, :], rel_a, to_up)
        far_down = remote(ps.at[0, hi, :], rel_b, to_down)
        up_hi = remote(ps.at[1, hi, :], from_minus.at[hi, :], to_up)
        down_lo = remote(ps.at[2, lo, :], from_plus.at[lo, :], to_down)
        up_lo = remote(ps.at[1, lo, :], from_minus.at[lo, :], to_up)
        down_hi = remote(ps.at[2, hi, :], from_plus.at[hi, :], to_down)

        terms = both(0)
        add_up(ps.at[0], 0, B, terms)
        far_up.start()
        far_down.start()
        terms = both(1)
        add_up(ps.at[1], HALF, HALF, terms)
        up_hi.start()
        terms_down = both(2)
        add_up(ps.at[2], 0, HALF, terms_down)
        down_lo.start()
        far_up.wait_recv()
        add_up(ps.at[1], 0, HALF, terms + (lambda at: rel_a[at, :],))
        up_lo.start()
        far_down.wait_recv()
        add_up(
            ps.at[2], HALF, HALF,
            terms_down + (lambda at: rel_b[span(at.start - HALF, chunk), :],),
        )
        down_hi.start()

        left_move.wait_recv()
        left_own.wait()
        left_gather = Gather(left_full)
        left_gather.start()

        terms = both(3)
        for copy in (up_hi, down_lo, up_lo, down_hi):
            copy.wait_recv()
        add_up(
            grad, 0, B, terms + (lambda at: from_minus[at, :], lambda at: from_plus[at, :])
        )

    with jax.named_scope("spread"):
        grad_move = Exchange(
            lambda p: grad.at[span(p * ROWS, ROWS), :], lambda rows: grad_cols.at[rows, :], ROWS
        )
        grad_move.start()
        grad_cols[own_rows, :] = grad[own_rows, :]

        def to_blocks(b, carry):
            by_block[b] = grad[span(b * ROWS, ROWS), :]
            return carry

        lax.fori_loop(0, OWNERS, to_blocks, 0)
        slot_moves = []
        for k in range(CAP):

            def pack(o, carry, k=k):
                q = o * CAP + k
                picked = by_block[ids_ref[q]].astype(F32)
                packed[k, span(o * ROWS, ROWS), :] = (picked * mask[pl.ds(q, 1), :]).astype(BF16)
                return carry

            lax.fori_loop(0, OWNERS, pack, 0)
            move = Exchange(
                lambda p, k=k: packed.at[k, span(p * ROWS, ROWS), :],
                lambda rows, k=k: slots.at[k, rows, own_cols], ROWS,
            )
            move.start()
            slots[k, own_rows, own_cols] = packed[k, own_rows, :]
            slot_moves.append(move)

    left_gather.relay_one()
    with jax.named_scope("moments"):
        m_in.wait()
        v_in.wait()

        def adam(b, carry):
            at = span(b * ROWS, ROWS)
            m_new, v_new, direction = adam_direction(
                grad[at, :].astype(F32), m_buf[at, :], v_buf[at, :]
            )
            m_buf[at, :] = m_new
            v_buf[at, :] = v_new
            sums[pl.ds(b, 1), :] = jnp.sum(direction * direction, axis=0, keepdims=True)
            return carry

        lax.fori_loop(0, OWNERS, adam, 0)
        m_done = local(m_buf, m_out)
        v_done = local(v_buf, v_out)
    left_gather.relay_two()
    left_gather.relay_three()
    left_gather.finish()

    def product(target, lhs, rhs):
        def one(i, carry):
            at = span(i * 256, 256)
            target(
                at, jnp.dot(lhs[at, :], rhs, preferred_element_type=F32)
            )
            return carry

        lax.fori_loop(0, B // 256, one, 0)

    with jax.named_scope("mixed"):
        grad_move.wait_recv()

        def keep_mixed(at, value):
            mixed_full[at, own_cols] = value.astype(BF16)

        product(keep_mixed, left_full, grad_cols[...])
        mixed_gather = Gather(mixed_full)
        mixed_gather.start()
        mixed_gather.relay_one()
    slot_gathers = [Gather(slots.at[k]) for k in range(CAP)]
    slot_moves[0].wait_recv()
    slot_gathers[0].start()
    mixed_gather.relay_two()
    mixed_gather.relay_three()
    slot_gathers[0].relay_one()
    mixed_gather.finish()

    with jax.named_scope("precond"):
        right_move.wait_recv()
        right_own.wait()
        tile_one[...] = jnp.zeros_like(tile_one)
        rhs_right = right_cols[...]

        def one(i, total):
            at = span(i * 256, 256)
            value = jnp.dot(mixed_full[at, :], rhs_right, preferred_element_type=F32)
            pre_half[at, :] = value.astype(BF16)
            return total + jnp.sum(value * value, axis=0, keepdims=True)

        square = lax.fori_loop(0, B // 256, one, jnp.zeros((1, WIDTH), F32))
        norm = jnp.sum(square, axis=1, keepdims=True)
        lane = lax.broadcasted_iota(jnp.int32, (8, 128), 1)
        line = lax.broadcasted_iota(jnp.int32, (8, 128), 0)
        block_sums = jnp.sum(sums[...], axis=1, keepdims=True)
        rows_id = lax.broadcasted_iota(jnp.int32, (OWNERS, 128), 0)
        lanes_id = lax.broadcasted_iota(jnp.int32, (OWNERS, 128), 1)
        adam_row = jnp.sum(jnp.where(rows_id == lanes_id, block_sums, 0.0), axis=0, keepdims=True)
        shampoo_tile = jnp.where((line == 0) & (lane == s), norm, 0.0)
        tile = jnp.where(line == 1, adam_row, shampoo_tile)
        tile_one[...] = tile
        norm_one[span(s * 8, 8), :] = tile
        norm_move = Exchange(lambda p: tile_one, lambda rows: norm_one.at[rows, :], 8)
        norm_move.start()
        back_move = Exchange(
            lambda p: pre_half.at[span(p * ROWS, ROWS), :],
            lambda rows: pre_tile.at[rows, :], ROWS,
        )
        back_move.start()
        pre_tile[own_rows, :] = pre_half[own_rows, :]

    ls_in.wait()
    rs_in.wait()
    stat_done = []

    def grams(k):
        with jax.named_scope("grams"):
            row_block = slots[k, own_cols, :]

            def left(i, carry):
                at = span(i * 256, 256)
                gram = lax.dot_general(
                    slots[k, at, :], row_block, (((1,), (1,)), ((), ())),
                    preferred_element_type=F32,
                )
                ls_buf[k, at, :] = BETA_STAT * ls_buf[k, at, :] + (1.0 - BETA_STAT) * gram
                return carry

            lax.fori_loop(0, B // 256, left, 0)
            stat_done.append(local(ls_buf.at[k], left_out.at[k]))
            flipped = slots[k, :, own_cols].T

            def right(i, carry):
                at = span(i * 256, 256)
                gram = jnp.dot(flipped, slots[k, :, at], preferred_element_type=F32).T
                rs_buf[k, at, :] = BETA_STAT * rs_buf[k, at, :] + (1.0 - BETA_STAT) * gram
                return carry

            lax.fori_loop(0, B // 256, right, 0)
            stat_done.append(local(rs_buf.at[k], right_out.at[k]))

    slot_gathers[0].relay_two()
    slot_moves[1].wait_recv()
    slot_gathers[1].start()
    slot_gathers[0].relay_three()

    with jax.named_scope("norms"):
        norm_move.wait_recv()
        half_sum = jnp.sum(norm_one[...].reshape(OWNERS, 8, 128), axis=0)
        tile_two[...] = half_sum
        norm_two[span(j * 8, 8), :] = half_sum
        send, recv = new_sem()

        def share(q, carry):
            other = lax.rem(j + q, GROUP)
            pltpu.make_async_remote_copy(
                src_ref=tile_two, dst_ref=norm_two.at[span(j * 8, 8), :], send_sem=send,
                recv_sem=recv,
                device_id={"tensor": other // 2, "section": lax.rem(other, 2)},
                device_id_type=MESH,
            ).start()
            return carry

        lax.fori_loop(1, GROUP, share, 0)
        seven = norm_two.at[pl.ds(0, (GROUP - 1) * 8), :]
        shared = Copy(seven, seven, send, recv, to_mate)
        sent.append(shared)

    slot_gathers[1].relay_one()
    slot_gathers[0].finish()
    grams(0)

    with jax.named_scope("update"):
        shared.wait_recv()
        totals = jnp.sum(norm_two[...].reshape(GROUP, 8, 128), axis=0)
        same_value = same[...]
        shampoo = jnp.sum(same_value * totals[0:1, :], axis=1, keepdims=True)
        adam_sum = jnp.sum(same_value * totals[1:2, :], axis=1, keepdims=True)
        counts = jnp.sum(same_value, axis=1, keepdims=True) * float(B * B)
        scale = jnp.sqrt(adam_sum / (shampoo + FLOOR_RATE * counts))
        scales[...] = jnp.broadcast_to(scale, (OWNERS, 128))
        back_move.wait_recv()
        w_in.wait()

        def update(b, carry):
            at = span(b * ROWS, ROWS)
            value = w_buf[at, :].astype(F32)
            step = scales[pl.ds(b, 1), :] * pre_tile[at, :].astype(F32)
            new_full[at, own_cols] = (value - LEARNING * (step + DECAY_RATE * value)).astype(BF16)
            return carry

        lax.fori_loop(0, OWNERS, update, 0)
        new_gather = Gather(new_full)
        new_gather.start()
    slot_gathers[1].relay_two()
    new_gather.relay_one()
    slot_moves[2].wait_recv()
    slot_gathers[2].start()
    slot_gathers[1].relay_three()
    new_gather.relay_two()
    new_gather.relay_three()
    slot_gathers[1].finish()
    slot_gathers[2].relay_one()
    grams(1)
    new_gather.finish()
    new_done = local(new_full, new_w)
    slot_gathers[2].relay_two()
    slot_gathers[2].relay_three()
    slot_gathers[2].finish()
    grams(2)

    for copy in sent:
        copy.wait_send()
    for copy in [m_done, v_done, new_done] + stat_done:
        copy.wait()


def fused_step(ids, parts, weights, m, v, left_stat, right_stat, left_root, right_root, mask, same):
    hbm = pl.BlockSpec(memory_space=pl.ANY)
    vmem = pl.BlockSpec(memory_space=pltpu.VMEM)
    smem = pl.BlockSpec(memory_space=pltpu.SMEM)
    slab = (B, WIDTH)
    full = (B, B)
    return pl.pallas_call(
        kernel,
        out_shape=(
            jax.ShapeDtypeStruct(full, BF16),
            jax.ShapeDtypeStruct(slab, F32),
            jax.ShapeDtypeStruct(slab, F32),
            jax.ShapeDtypeStruct((CAP,) + slab, F32),
            jax.ShapeDtypeStruct((CAP,) + slab, F32),
        ),
        in_specs=[smem] + [hbm] * 8 + [vmem] * 2,
        out_specs=(hbm,) * 5,
        scratch_shapes=[
            pltpu.VMEM((RING,) + slab, BF16),
            pltpu.VMEM((RING,) + slab, BF16),
            pltpu.VMEM((3,) + slab, BF16),
            pltpu.VMEM((HALF, WIDTH), BF16),
            pltpu.VMEM((HALF, WIDTH), BF16),
            pltpu.VMEM(slab, BF16),
            pltpu.VMEM(slab, BF16),
            pltpu.VMEM(slab, BF16),
            pltpu.VMEM((OWNERS, ROWS, WIDTH), BF16),
            pltpu.VMEM((CAP,) + slab, BF16),
            pltpu.VMEM(full, BF16),
            pltpu.VMEM(full, BF16),
            pltpu.VMEM(full, BF16),
            pltpu.VMEM((CAP,) + full, BF16),
            pltpu.VMEM(slab, BF16),
            pltpu.VMEM(slab, BF16),
            pltpu.VMEM(slab, BF16),
            pltpu.VMEM(slab, BF16),
            pltpu.VMEM(slab, BF16),
            pltpu.VMEM(slab, F32),
            pltpu.VMEM(slab, F32),
            pltpu.VMEM((CAP,) + slab, F32),
            pltpu.VMEM((CAP,) + slab, F32),
            pltpu.VMEM((8, 128), F32),
            pltpu.VMEM((OWNERS * 8, 128), F32),
            pltpu.VMEM((8, 128), F32),
            pltpu.VMEM((GROUP * 8, 128), F32),
            pltpu.VMEM((OWNERS, 128), F32),
            pltpu.VMEM((OWNERS, 128), F32),
            pltpu.SemaphoreType.DMA((96,)),
            pltpu.SemaphoreType.DMA((96,)),
            pltpu.SemaphoreType.DMA((32,)),
        ],
        compiler_params=pltpu.CompilerParams(
            collective_id=0, has_side_effects=True, vmem_limit_bytes=56 * 2**20
        ),
        name="shampoo_step",
    )(ids, parts, weights, m, v, left_stat, right_stat, left_root, right_root, mask, same)


def shards(
    grad_parts,
    weights,
    adam_m,
    adam_v,
    left_stat,
    right_stat,
    left_root,
    right_root,
    block_owner,
    block_matrix,
    factors,
    factor_grad,
    factor_m,
    factor_v,
):
    slot = slot_numbers(block_owner, CAP)
    block_ids, occupied = slot_contents(slot, OWNERS * CAP)
    mask = jnp.broadcast_to(occupied.astype(F32)[:, None], (OWNERS * CAP, 128))
    same = jnp.pad(
        (block_matrix[:, None] == block_matrix[None, :]).astype(F32), ((0, 0), (0, 128 - OWNERS))
    )
    new_weights, adam_m_new, adam_v_new, left_new, right_new = fused_step(
        block_ids,
        grad_parts.reshape(B, B),
        weights.reshape(B, WIDTH),
        adam_m.reshape(B, WIDTH),
        adam_v.reshape(B, WIDTH),
        left_stat,
        right_stat,
        left_root.reshape(B, WIDTH),
        right_root.reshape(B, WIDTH),
        mask,
        same,
    )
    factor_m_new, factor_v_new, factor_step = adam_direction(
        factor_grad.astype(F32), factor_m, factor_v
    )
    factors_new = factors - LEARNING * (factor_step + DECAY_RATE * factors)
    return (
        new_weights.reshape(OWNERS, ROWS, B),
        adam_m_new.reshape(OWNERS, ROWS, WIDTH),
        adam_v_new.reshape(OWNERS, ROWS, WIDTH),
        left_new,
        right_new,
        factors_new,
        factor_m_new,
        factor_v_new,
    )


def solution(mesh):
    row = ("tensor", "section")
    slab = P(None, "shard", row)
    stat = P("shard", None, row)
    factor = P("shard", row)
    in_specs = (
        P(row, None, "shard", None), slab, slab, slab, stat, stat, slab, slab, P(), P(),
        factor, factor, factor, factor,
    )
    out_specs = (P(None, "shard", None), slab, slab, stat, stat, factor, factor, factor)
    return jax.shard_map(shards, mesh=mesh, in_specs=in_specs, out_specs=out_specs, check_vma=False)
```

```python
import jax
import jax.numpy as jnp
from jax import lax
from jax.experimental import pallas as pl
from jax.experimental.pallas import tpu as pltpu
from jax.sharding import PartitionSpec as P

B = 1024
MATS = 5

BETA_ONE = 0.9
BETA_TWO = 0.95
BETA_STAT = 0.95
LEARNING = 0.1
DECAY_RATE = 0.1
EPSILON = 1e-08
FLOOR_RATE = 1e-06
CORRECT_ONE = 1.0 - 0.9**10
CORRECT_TWO = 1.0 - 0.95**10

MESH = pl.DeviceIdType.MESH
F32 = jnp.float32
BF16 = jnp.bfloat16
OWNERS = 32
RING = 4
GROUP = 8
ROWS = B // OWNERS
WIDTH = B // GROUP
HALF = B // 2
CAP = 3
NONE = OWNERS
VMEM_LIMIT = 34 * 2**20
WRITE_LIMIT = 16 * 2**20


def adam_direction(grad_float, moment, second):
    moment_new = BETA_ONE * moment + (1.0 - BETA_ONE) * grad_float
    second_new = BETA_TWO * second + (1.0 - BETA_TWO) * grad_float * grad_float
    direction = moment_new / CORRECT_ONE / (jnp.sqrt(second_new / CORRECT_TWO) + EPSILON)
    return (moment_new, second_new, direction)


def slot_blocks(block_owner):
    positions = jnp.arange(OWNERS, dtype=jnp.int32)
    earlier = (block_owner[:, None] == block_owner[None, :]) & (
        positions[None, :] < positions[:, None]
    )
    slot = block_owner * CAP + jnp.sum(earlier.astype(jnp.int32), axis=1)
    matches = jnp.arange(OWNERS * CAP, dtype=jnp.int32)[:, None] == slot[None, :]
    return NONE + jnp.sum(jnp.where(matches, positions[None, :] - NONE, 0), axis=1)


class Copy:
    def __init__(self, src, dst, send, recv, target, landing=None):
        self.out = pltpu.make_async_remote_copy(
            src_ref=src, dst_ref=dst, send_sem=send, recv_sem=recv, device_id=target,
            device_id_type=MESH,
        )
        here = dst if landing is None else landing
        self.into = pltpu.make_async_remote_copy(
            src_ref=here, dst_ref=here, send_sem=send, recv_sem=recv, device_id=target,
            device_id_type=MESH,
        )

    def start(self):
        self.out.start()

    def wait_recv(self):
        self.into.wait_recv()

    def wait_send(self):
        self.out.wait_send()


def span(start, size):
    return pl.ds(pl.multiple_of(start, size), size)


def kernel(
    ids_ref, matrix_ref, parts, weights, adam_m, adam_v, left_stat, right_stat, left_root, right_root,
    new_full, m_buf, v_buf, ls_buf, rs_buf,
    mine, pre, ps, rel_a, rel_b, from_minus, from_plus, grad, by_block, packed, left_full, mixed_full,
    slots, grad_cols, right_cols, pre_half, pre_tile, w_buf, tile_one, norm_one, tile_two, norm_two, sums, scales,
    send_sem, recv_sem, local_sem,
):
    s = lax.axis_index("shard")
    t = lax.axis_index("tensor")
    c = lax.axis_index("section")
    j = t * 2 + c
    up, down, across = lax.rem(t + 1, RING), lax.rem(t + 3, RING), lax.rem(t + 2, RING)
    to_up, to_down = {"tensor": up}, {"tensor": down}
    to_mate = {"section": 1 - c}
    own_cols = span(j * WIDTH, WIDTH)
    own_rows = span(s * ROWS, ROWS)
    counters = {"sem": 0, "local": 0}
    sent = []

    def new_sem():
        index = counters["sem"]
        counters["sem"] += 1
        return send_sem.at[index], recv_sem.at[index]

    def local(src, dst):
        index = counters["local"]
        counters["local"] += 1
        copy = pltpu.make_async_copy(src, dst, local_sem.at[index])
        copy.start()
        return copy

    def remote(src, dst, target, landing=None):
        send, recv = new_sem()
        copy = Copy(src, dst, send, recv, target, landing)
        sent.append(copy)
        return copy

    class Exchange:
        def __init__(self, src, dst, size, fixed=False):
            self.src, self.dst, self.size, self.fixed = src, dst, size, fixed
            self.send, self.recv = new_sem()
            whole = dst(pl.ds(0, (OWNERS - 1) * size))
            self.all = pltpu.make_async_remote_copy(
                src_ref=whole, dst_ref=whole, send_sem=self.send, recv_sem=self.recv,
                device_id={"shard": lax.rem(s + 1, OWNERS)}, device_id_type=MESH,
            )
            sent.append(self)

        def start(self):
            def one(k, carry):
                p = lax.rem(s + k, OWNERS)
                pltpu.make_async_remote_copy(
                    src_ref=self.src(p), dst_ref=self.dst(span(s * self.size, self.size)),
                    send_sem=self.send, recv_sem=self.recv, device_id={"shard": p},
                    device_id_type=MESH,
                ).start()
                return carry

            lax.fori_loop(1, OWNERS, one, 0)

        def wait_recv(self):
            self.all.wait_recv()

        def wait_send(self):
            self.all.wait_send()

    class Gather:
        def __init__(self, full):
            def part(slab, first, size):
                return full.at[pl.ds(first, size), span(slab * WIDTH, WIDTH)]

            own = j
            below, above, far = down * 2 + c, up * 2 + c, across * 2 + c
            lo, hi = (0, HALF), (HALF, HALF)
            self.up_lo = remote(part(own, *lo), part(own, *lo), to_up, part(below, *lo))
            self.up_hi = remote(part(own, *hi), part(own, *hi), to_up, part(below, *hi))
            self.down_hi = remote(part(own, *hi), part(own, *hi), to_down, part(above, *hi))
            self.down_lo = remote(part(own, *lo), part(own, *lo), to_down, part(above, *lo))
            self.fwd_up = remote(part(below, *lo), part(below, *lo), to_up, part(far, *lo))
            self.fwd_down = remote(part(above, *hi), part(above, *hi), to_down, part(far, *hi))
            mates = []
            for row in (t, down, up, across):
                mates.append(
                    remote(
                        part(row * 2 + c, 0, B), part(row * 2 + c, 0, B), to_mate,
                        part(row * 2 + 1 - c, 0, B),
                    )
                )
            self.mates = mates

        def start(self):
            self.up_lo.start()
            self.down_hi.start()
            self.up_hi.start()
            self.down_lo.start()
            self.mates[0].start()

        def relay_one(self):
            self.up_lo.wait_recv()
            self.fwd_up.start()
            self.down_hi.wait_recv()
            self.fwd_down.start()

        def relay_two(self):
            self.up_hi.wait_recv()
            self.mates[1].start()
            self.down_lo.wait_recv()
            self.mates[2].start()

        def relay_three(self):
            self.fwd_up.wait_recv()
            self.fwd_down.wait_recv()
            self.mates[3].start()

        def finish(self):
            for mate in self.mates:
                mate.wait_recv()

    with jax.named_scope("entry"):
        barrier = pltpu.get_barrier_semaphore()

        def greet(k, carry):
            pl.semaphore_signal(
                barrier, inc=1, device_id={"shard": lax.rem(s + k, OWNERS)}, device_id_type=MESH
            )
            return carry

        lax.fori_loop(1, OWNERS, greet, 0)

        def greet_row(q, carry):
            other = lax.rem(j + q, GROUP)
            pl.semaphore_signal(
                barrier, inc=1, device_id={"tensor": other // 2, "section": lax.rem(other, 2)},
                device_id_type=MESH,
            )
            return carry

        lax.fori_loop(1, GROUP, greet_row, 0)

        order = (across, up, down, t)
        mine_in = []
        for slot, row in enumerate(order):
            mine_in.append(
                local(parts.at[:, span((row * 2 + c) * WIDTH, WIDTH)], mine.at[slot])
            )
        right_own = local(right_root.at[own_rows, :], right_cols.at[own_rows, :])
        left_own = local(left_root.at[own_rows, :], left_full.at[own_rows, own_cols])
        m_in = local(adam_m, m_buf)
        v_in = local(adam_v, v_buf)
        w_in = local(weights, w_buf)
        ls_in = local(left_stat, ls_buf)
        rs_in = local(right_stat, rs_buf)
        pl.semaphore_wait(barrier, OWNERS - 1 + GROUP - 1)

    with jax.named_scope("reduce"):
        pairs = []
        for slot, row in enumerate(order):
            pairs.append(
                remote(
                    parts.at[:, span((row * 2 + 1 - c) * WIDTH, WIDTH)], pre.at[slot], to_mate
                )
            )
        for pair in pairs:
            pair.start()
        left_move = Exchange(
            lambda p: left_root.at[span(p * ROWS, ROWS), :],
            lambda rows: left_full.at[rows, own_cols], ROWS,
        )
        right_move = Exchange(
            lambda p: right_root.at[span(p * ROWS, ROWS), :],
            lambda rows: right_cols.at[rows, :], ROWS,
        )
        left_move.start()
        right_move.start()

        lo, hi = pl.ds(0, HALF), pl.ds(HALF, HALF)
        chunk = 64

        def add_up(target, first, rows, terms):
            def one(i, carry):
                at = span(first + i * chunk, chunk)
                total = terms[0](at).astype(F32)
                for term in terms[1:]:
                    total = total + term(at).astype(F32)
                target[at, :] = total.astype(BF16)
                return carry

            lax.fori_loop(0, rows // chunk, one, 0)

        def both(slot):
            mine_in[slot].wait()
            pairs[slot].wait_recv()
            return (lambda at: mine[slot, at, :], lambda at: pre[slot, at, :])

        far_up = remote(ps.at[0, lo, :], rel_a, to_up)
        far_down = remote(ps.at[0, hi, :], rel_b, to_down)
        up_hi = remote(ps.at[1, hi, :], from_minus.at[hi, :], to_up)
        down_lo = remote(ps.at[2, lo, :], from_plus.at[lo, :], to_down)
        up_lo = remote(ps.at[1, lo, :], from_minus.at[lo, :], to_up)
        down_hi = remote(ps.at[2, hi, :], from_plus.at[hi, :], to_down)

        terms = both(0)
        add_up(ps.at[0], 0, B, terms)
        far_up.start()
        far_down.start()
        terms = both(1)
        add_up(ps.at[1], HALF, HALF, terms)
        up_hi.start()
        terms_down = both(2)
        add_up(ps.at[2], 0, HALF, terms_down)
        down_lo.start()
        far_up.wait_recv()
        add_up(ps.at[1], 0, HALF, terms + (lambda at: rel_a[at, :],))
        up_lo.start()
        far_down.wait_recv()
        add_up(
            ps.at[2], HALF, HALF,
            terms_down + (lambda at: rel_b[span(at.start - HALF, chunk), :],),
        )
        down_hi.start()

        left_move.wait_recv()
        left_own.wait()
        left_gather = Gather(left_full)
        left_gather.start()

        terms = both(3)
        for copy in (up_hi, down_lo, up_lo, down_hi):
            copy.wait_recv()
        add_up(
            grad, 0, B, terms + (lambda at: from_minus[at, :], lambda at: from_plus[at, :])
        )

    with jax.named_scope("spread"):
        grad_move = Exchange(
            lambda p: grad.at[span(p * ROWS, ROWS), :], lambda rows: grad_cols.at[rows, :], ROWS
        )
        grad_move.start()
        grad_cols[own_rows, :] = grad[own_rows, :]

        def to_blocks(b, carry):
            by_block[b] = grad[span(b * ROWS, ROWS), :]
            return carry

        lax.fori_loop(0, OWNERS, to_blocks, 0)
        by_block[NONE] = jnp.zeros((ROWS, WIDTH), BF16)
        slot_moves = []
        for k in range(CAP):

            def pack(o, carry, k=k):
                q = o * CAP + k
                packed[k, span(o * ROWS, ROWS), :] = by_block[ids_ref[q]]
                return carry

            lax.fori_loop(0, OWNERS, pack, 0)
            move = Exchange(
                lambda p, k=k: packed.at[k, span(p * ROWS, ROWS), :],
                lambda rows, k=k: slots.at[k, rows, own_cols], ROWS,
            )
            move.start()
            slots[k, own_rows, own_cols] = packed[k, own_rows, :]
            slot_moves.append(move)

    left_gather.relay_one()
    with jax.named_scope("moments"):
        m_in.wait()
        v_in.wait()

        def adam(b, carry):
            at = span(b * ROWS, ROWS)
            m_new, v_new, direction = adam_direction(
                grad[at, :].astype(F32), m_buf[at, :], v_buf[at, :]
            )
            m_buf[at, :] = m_new
            v_buf[at, :] = v_new
            sums[pl.ds(b, 1), :] = jnp.sum(direction * direction, axis=0, keepdims=True)
            return carry

        lax.fori_loop(0, OWNERS, adam, 0)
    left_gather.relay_two()
    left_gather.relay_three()
    left_gather.finish()

    def product(target, lhs, rhs):
        def one(i, carry):
            at = span(i * 256, 256)
            target(
                at, jnp.dot(lhs[at, :], rhs, preferred_element_type=F32)
            )
            return carry

        lax.fori_loop(0, B // 256, one, 0)

    with jax.named_scope("mixed"):
        grad_move.wait_recv()

        def keep_mixed(at, value):
            mixed_full[at, own_cols] = value.astype(BF16)

        product(keep_mixed, left_full, grad_cols[...])
        mixed_gather = Gather(mixed_full)
        mixed_gather.start()
        mixed_gather.relay_one()
    slot_gathers = [Gather(slots.at[k]) for k in range(CAP)]
    slot_moves[0].wait_recv()
    slot_gathers[0].start()
    mixed_gather.relay_two()
    mixed_gather.relay_three()
    slot_gathers[0].relay_one()
    mixed_gather.finish()

    with jax.named_scope("precond"):
        right_move.wait_recv()
        right_own.wait()
        tile_one[...] = jnp.zeros_like(tile_one)
        rhs_right = right_cols[...]

        def one(i, total):
            at = span(i * 256, 256)
            value = jnp.dot(mixed_full[at, :], rhs_right, preferred_element_type=F32)
            pre_half[at, :] = value.astype(BF16)
            return total + jnp.sum(value * value, axis=0, keepdims=True)

        square = lax.fori_loop(0, B // 256, one, jnp.zeros((1, WIDTH), F32))
        norm = jnp.sum(square, axis=1, keepdims=True)
        lane = lax.broadcasted_iota(jnp.int32, (8, 128), 1)
        line = lax.broadcasted_iota(jnp.int32, (8, 128), 0)
        block_sums = jnp.sum(sums[...], axis=1, keepdims=True)
        rows_id = lax.broadcasted_iota(jnp.int32, (OWNERS, 128), 0)
        lanes_id = lax.broadcasted_iota(jnp.int32, (OWNERS, 128), 1)
        adam_row = jnp.sum(jnp.where(rows_id == lanes_id, block_sums, 0.0), axis=0, keepdims=True)
        shampoo_tile = jnp.where((line == 0) & (lane == s), norm, 0.0)
        tile = jnp.where(line == 1, adam_row, shampoo_tile)
        tile_one[...] = tile
        norm_one[span(s * 8, 8), :] = tile
        norm_move = Exchange(lambda p: tile_one, lambda rows: norm_one.at[rows, :], 8)
        norm_move.start()
        back_move = Exchange(
            lambda p: pre_half.at[span(p * ROWS, ROWS), :],
            lambda rows: pre_tile.at[rows, :], ROWS,
        )
        back_move.start()
        pre_tile[own_rows, :] = pre_half[own_rows, :]

    ls_in.wait()
    rs_in.wait()

    def grams(k):
        with jax.named_scope("grams"):
            row_block = slots[k, own_cols, :]

            def left(i, carry):
                at = span(i * 256, 256)
                gram = lax.dot_general(
                    slots[k, at, :], row_block, (((1,), (1,)), ((), ())),
                    preferred_element_type=F32,
                )
                ls_buf[k, at, :] = BETA_STAT * ls_buf[k, at, :] + (1.0 - BETA_STAT) * gram
                return carry

            lax.fori_loop(0, B // 256, left, 0)
            flipped = slots[k, :, own_cols].T

            def right(i, carry):
                at = span(i * 256, 256)
                gram = jnp.dot(flipped, slots[k, :, at], preferred_element_type=F32).T
                rs_buf[k, at, :] = BETA_STAT * rs_buf[k, at, :] + (1.0 - BETA_STAT) * gram
                return carry

            lax.fori_loop(0, B // 256, right, 0)

    slot_gathers[0].relay_two()
    slot_moves[1].wait_recv()
    slot_gathers[1].start()
    slot_gathers[0].relay_three()

    with jax.named_scope("norms"):
        norm_move.wait_recv()
        half_sum = jnp.sum(norm_one[...].reshape(OWNERS, 8, 128), axis=0)
        tile_two[...] = half_sum
        norm_two[span(j * 8, 8), :] = half_sum
        send, recv = new_sem()

        def share(q, carry):
            other = lax.rem(j + q, GROUP)
            pltpu.make_async_remote_copy(
                src_ref=tile_two, dst_ref=norm_two.at[span(j * 8, 8), :], send_sem=send,
                recv_sem=recv,
                device_id={"tensor": other // 2, "section": lax.rem(other, 2)},
                device_id_type=MESH,
            ).start()
            return carry

        lax.fori_loop(1, GROUP, share, 0)
        seven = norm_two.at[pl.ds(0, (GROUP - 1) * 8), :]
        shared = Copy(seven, seven, send, recv, to_mate)
        sent.append(shared)

    slot_gathers[1].relay_one()
    slot_gathers[0].finish()
    grams(0)

    with jax.named_scope("update"):
        shared.wait_recv()
        totals = jnp.sum(norm_two[...].reshape(GROUP, 8, 128), axis=0)
        names_down = jnp.zeros((OWNERS, 128), jnp.int32)
        names_along = jnp.full((OWNERS, 128), -1, jnp.int32)
        for b in range(OWNERS):
            names_down = jnp.where(rows_id == b, matrix_ref[b], names_down)
            names_along = jnp.where(lanes_id == b, matrix_ref[b], names_along)
        same_value = (names_down == names_along).astype(F32)
        shampoo = jnp.sum(same_value * totals[0:1, :], axis=1, keepdims=True)
        adam_sum = jnp.sum(same_value * totals[1:2, :], axis=1, keepdims=True)
        counts = jnp.sum(same_value, axis=1, keepdims=True) * float(B * B)
        scale = jnp.sqrt(adam_sum / (shampoo + FLOOR_RATE * counts))
        scales[...] = jnp.broadcast_to(scale, (OWNERS, 128))
        back_move.wait_recv()
        w_in.wait()

        def update(b, carry):
            at = span(b * ROWS, ROWS)
            value = w_buf[at, :].astype(F32)
            step = scales[pl.ds(b, 1), :] * pre_tile[at, :].astype(F32)
            new_full[at, own_cols] = (value - LEARNING * (step + DECAY_RATE * value)).astype(BF16)
            return carry

        lax.fori_loop(0, OWNERS, update, 0)
        new_gather = Gather(new_full)
        new_gather.start()
    slot_gathers[1].relay_two()
    new_gather.relay_one()
    slot_moves[2].wait_recv()
    slot_gathers[2].start()
    slot_gathers[1].relay_three()
    new_gather.relay_two()
    new_gather.relay_three()
    slot_gathers[1].finish()
    slot_gathers[2].relay_one()
    grams(1)
    new_gather.finish()
    slot_gathers[2].relay_two()
    slot_gathers[2].relay_three()
    slot_gathers[2].finish()
    grams(2)

    for copy in sent:
        copy.wait_send()


def fused_step(ids, matrix, parts, weights, m, v, left_stat, right_stat, left_root, right_root):
    hbm = pl.BlockSpec(memory_space=pltpu.HBM)
    vmem = pl.BlockSpec(memory_space=pltpu.VMEM)
    smem = pl.BlockSpec(memory_space=pltpu.SMEM)
    slab = (B, WIDTH)
    full = (B, B)
    shapes = (
        jax.ShapeDtypeStruct(full, BF16),
        jax.ShapeDtypeStruct(slab, F32),
        jax.ShapeDtypeStruct(slab, F32),
        jax.ShapeDtypeStruct((CAP,) + slab, F32),
        jax.ShapeDtypeStruct((CAP,) + slab, F32),
    )
    stay = [
        pltpu.with_memory_space_constraint(x, pltpu.HBM)
        for x in (parts, weights, m, v, left_stat, right_stat, left_root, right_root)
    ]
    results = pl.pallas_call(
        kernel,
        out_shape=tuple(pltpu.VMEM(x.shape, x.dtype) for x in shapes),
        in_specs=[smem] * 2 + [hbm] * 8,
        out_specs=(vmem,) * 5,
        scratch_shapes=[
            pltpu.VMEM((RING,) + slab, BF16),
            pltpu.VMEM((RING,) + slab, BF16),
            pltpu.VMEM((3,) + slab, BF16),
            pltpu.VMEM((HALF, WIDTH), BF16),
            pltpu.VMEM((HALF, WIDTH), BF16),
            pltpu.VMEM(slab, BF16),
            pltpu.VMEM(slab, BF16),
            pltpu.VMEM(slab, BF16),
            pltpu.VMEM((OWNERS + 1, ROWS, WIDTH), BF16),
            pltpu.VMEM((CAP,) + slab, BF16),
            pltpu.VMEM(full, BF16),
            pltpu.VMEM(full, BF16),
            pltpu.VMEM((CAP,) + full, BF16),
            pltpu.VMEM(slab, BF16),
            pltpu.VMEM(slab, BF16),
            pltpu.VMEM(slab, BF16),
            pltpu.VMEM(slab, BF16),
            pltpu.VMEM(slab, BF16),
            pltpu.VMEM((8, 128), F32),
            pltpu.VMEM((OWNERS * 8, 128), F32),
            pltpu.VMEM((8, 128), F32),
            pltpu.VMEM((GROUP * 8, 128), F32),
            pltpu.VMEM((OWNERS, 128), F32),
            pltpu.VMEM((OWNERS, 128), F32),
            pltpu.SemaphoreType.DMA((96,)),
            pltpu.SemaphoreType.DMA((96,)),
            pltpu.SemaphoreType.DMA((32,)),
        ],
        compiler_params=pltpu.CompilerParams(
            collective_id=0, has_side_effects=True, vmem_limit_bytes=VMEM_LIMIT
        ),
        name="shampoo_step",
    )(ids, matrix, *stay)
    return pl.pallas_call(
        write_out,
        out_shape=shapes,
        in_specs=[vmem] * 5,
        out_specs=(hbm,) * 5,
        scratch_shapes=[pltpu.SemaphoreType.DMA((5,))],
        compiler_params=pltpu.CompilerParams(vmem_limit_bytes=WRITE_LIMIT),
        name="write_out",
    )(*results)


def write_out(*refs):
    copies = [
        pltpu.make_async_copy(src, dst, refs[10].at[i])
        for i, (src, dst) in enumerate(zip(refs[:5], refs[5:10]))
    ]
    for copy in copies:
        copy.start()
    for copy in copies:
        copy.wait()


def shards(
    grad_parts,
    weights,
    adam_m,
    adam_v,
    left_stat,
    right_stat,
    left_root,
    right_root,
    block_owner,
    block_matrix,
    factors,
    factor_grad,
    factor_m,
    factor_v,
):
    block_ids = slot_blocks(block_owner)
    new_weights, adam_m_new, adam_v_new, left_new, right_new = fused_step(
        block_ids,
        block_matrix,
        grad_parts.reshape(B, B),
        weights.reshape(B, WIDTH),
        adam_m.reshape(B, WIDTH),
        adam_v.reshape(B, WIDTH),
        left_stat,
        right_stat,
        left_root.reshape(B, WIDTH),
        right_root.reshape(B, WIDTH),
    )
    factor_m_new, factor_v_new, factor_step = adam_direction(
        factor_grad.astype(F32), factor_m, factor_v
    )
    factors_new = factors - LEARNING * (factor_step + DECAY_RATE * factors)
    return (
        new_weights.reshape(OWNERS, ROWS, B),
        adam_m_new.reshape(OWNERS, ROWS, WIDTH),
        adam_v_new.reshape(OWNERS, ROWS, WIDTH),
        left_new,
        right_new,
        factors_new,
        factor_m_new,
        factor_v_new,
    )


def solution(mesh):
    row = ("tensor", "section")
    slab = P(None, "shard", row)
    stat = P("shard", None, row)
    factor = P("shard", row)
    in_specs = (
        P(row, None, "shard", None), slab, slab, slab, stat, stat, slab, slab, P(), P(),
        factor, factor, factor, factor,
    )
    out_specs = (P(None, "shard", None), slab, slab, stat, stat, factor, factor, factor)
    return jax.shard_map(shards, mesh=mesh, in_specs=in_specs, out_specs=out_specs, check_vma=False)
```

```python
import jax
import jax.numpy as jnp
from jax import lax
from jax.experimental import pallas as pl
from jax.experimental.pallas import tpu as pltpu
from jax.sharding import PartitionSpec as P

B = 1024
MATS = 5

BETA_ONE = 0.9
BETA_TWO = 0.95
BETA_STAT = 0.95
LEARNING = 0.1
DECAY_RATE = 0.1
EPSILON = 1e-08
FLOOR_RATE = 1e-06
CORRECT_ONE = 1.0 - 0.9**10
CORRECT_TWO = 1.0 - 0.95**10

MESH = pl.DeviceIdType.MESH
F32 = jnp.float32
BF16 = jnp.bfloat16
OWNERS = 32
RING = 4
GROUP = 8
ROWS = B // OWNERS
WIDTH = B // GROUP
HALF = B // 2
CAP = 3
NONE = OWNERS
VMEM_LIMIT = 34 * 2**20
WRITE_LIMIT = 16 * 2**20


def adam_direction(grad_float, moment, second):
    moment_new = BETA_ONE * moment + (1.0 - BETA_ONE) * grad_float
    second_new = BETA_TWO * second + (1.0 - BETA_TWO) * grad_float * grad_float
    direction = moment_new / CORRECT_ONE / (jnp.sqrt(second_new / CORRECT_TWO) + EPSILON)
    return (moment_new, second_new, direction)


def slot_blocks(block_owner):
    positions = jnp.arange(OWNERS, dtype=jnp.int32)
    earlier = (block_owner[:, None] == block_owner[None, :]) & (
        positions[None, :] < positions[:, None]
    )
    slot = block_owner * CAP + jnp.sum(earlier.astype(jnp.int32), axis=1)
    matches = jnp.arange(OWNERS * CAP, dtype=jnp.int32)[:, None] == slot[None, :]
    return NONE + jnp.sum(jnp.where(matches, positions[None, :] - NONE, 0), axis=1)


class Copy:
    def __init__(self, src, dst, send, recv, target, landing=None):
        self.out = pltpu.make_async_remote_copy(
            src_ref=src, dst_ref=dst, send_sem=send, recv_sem=recv, device_id=target,
            device_id_type=MESH,
        )
        here = dst if landing is None else landing
        self.into = pltpu.make_async_remote_copy(
            src_ref=here, dst_ref=here, send_sem=send, recv_sem=recv, device_id=target,
            device_id_type=MESH,
        )

    def start(self):
        self.out.start()

    def wait_recv(self):
        self.into.wait_recv()

    def wait_send(self):
        self.out.wait_send()


def span(start, size):
    return pl.ds(pl.multiple_of(start, size), size)


def kernel(
    ids_ref, matrix_ref, parts, weights, adam_m, adam_v, left_stat, right_stat, left_root, right_root,
    new_full, m_buf, v_buf, ls_buf, rs_buf,
    mine, pre, ps, rel_a, rel_b, from_minus, from_plus, grad, by_block, packed, left_full, mixed_full,
    slots, grad_cols, right_cols, pre_half, pre_tile, w_buf, tile_one, norm_one, tile_two, norm_two, sums, scales,
    send_sem, recv_sem, local_sem,
):
    s = lax.axis_index("shard")
    t = lax.axis_index("tensor")
    c = lax.axis_index("section")
    j = t * 2 + c
    up, down, across = lax.rem(t + 1, RING), lax.rem(t + 3, RING), lax.rem(t + 2, RING)
    to_up, to_down = {"tensor": up}, {"tensor": down}
    to_mate = {"section": 1 - c}
    own_cols = span(j * WIDTH, WIDTH)
    own_rows = span(s * ROWS, ROWS)
    counters = {"sem": 0, "local": 0}
    sent = []

    def new_sem():
        index = counters["sem"]
        counters["sem"] += 1
        return send_sem.at[index], recv_sem.at[index]

    def local(src, dst):
        index = counters["local"]
        counters["local"] += 1
        copy = pltpu.make_async_copy(src, dst, local_sem.at[index])
        copy.start()
        return copy

    def remote(src, dst, target, landing=None):
        send, recv = new_sem()
        copy = Copy(src, dst, send, recv, target, landing)
        sent.append(copy)
        return copy

    class Exchange:
        def __init__(self, src, dst, size, fixed=False):
            self.src, self.dst, self.size, self.fixed = src, dst, size, fixed
            self.send, self.recv = new_sem()
            whole = dst(pl.ds(0, (OWNERS - 1) * size))
            self.all = pltpu.make_async_remote_copy(
                src_ref=whole, dst_ref=whole, send_sem=self.send, recv_sem=self.recv,
                device_id={"shard": lax.rem(s + 1, OWNERS)}, device_id_type=MESH,
            )
            sent.append(self)

        def start(self):
            def one(k, carry):
                p = lax.rem(s + k, OWNERS)
                pltpu.make_async_remote_copy(
                    src_ref=self.src(p), dst_ref=self.dst(span(s * self.size, self.size)),
                    send_sem=self.send, recv_sem=self.recv, device_id={"shard": p},
                    device_id_type=MESH,
                ).start()
                return carry

            lax.fori_loop(1, OWNERS, one, 0)

        def wait_recv(self):
            self.all.wait_recv()

        def wait_send(self):
            self.all.wait_send()

    class Gather:
        def __init__(self, full):
            def part(slab, first, size):
                return full.at[pl.ds(first, size), span(slab * WIDTH, WIDTH)]

            own = j
            below, above, far = down * 2 + c, up * 2 + c, across * 2 + c
            lo, hi = (0, HALF), (HALF, HALF)
            self.up_lo = remote(part(own, *lo), part(own, *lo), to_up, part(below, *lo))
            self.up_hi = remote(part(own, *hi), part(own, *hi), to_up, part(below, *hi))
            self.down_hi = remote(part(own, *hi), part(own, *hi), to_down, part(above, *hi))
            self.down_lo = remote(part(own, *lo), part(own, *lo), to_down, part(above, *lo))
            self.fwd_up = remote(part(below, *lo), part(below, *lo), to_up, part(far, *lo))
            self.fwd_down = remote(part(above, *hi), part(above, *hi), to_down, part(far, *hi))
            mates = []
            for row in (t, down, up, across):
                mates.append(
                    remote(
                        part(row * 2 + c, 0, B), part(row * 2 + c, 0, B), to_mate,
                        part(row * 2 + 1 - c, 0, B),
                    )
                )
            self.mates = mates

        def start(self):
            self.up_lo.start()
            self.down_hi.start()
            self.up_hi.start()
            self.down_lo.start()
            self.mates[0].start()

        def relay_one(self):
            self.up_lo.wait_recv()
            self.fwd_up.start()
            self.down_hi.wait_recv()
            self.fwd_down.start()

        def relay_two(self):
            self.up_hi.wait_recv()
            self.mates[1].start()
            self.down_lo.wait_recv()
            self.mates[2].start()

        def relay_three(self):
            self.fwd_up.wait_recv()
            self.fwd_down.wait_recv()
            self.mates[3].start()

        def finish(self):
            for mate in self.mates:
                mate.wait_recv()

    with jax.named_scope("entry"):
        barrier = pltpu.get_barrier_semaphore()

        def greet(k, carry):
            pl.semaphore_signal(
                barrier, inc=1, device_id={"shard": lax.rem(s + k, OWNERS)}, device_id_type=MESH
            )
            return carry

        lax.fori_loop(1, OWNERS, greet, 0)

        def greet_row(q, carry):
            other = lax.rem(j + q, GROUP)
            pl.semaphore_signal(
                barrier, inc=1, device_id={"tensor": other // 2, "section": lax.rem(other, 2)},
                device_id_type=MESH,
            )
            return carry

        lax.fori_loop(1, GROUP, greet_row, 0)

        order = (across, up, down, t)
        mine_in = []
        for slot, row in enumerate(order):
            mine_in.append(
                local(parts.at[:, span((row * 2 + c) * WIDTH, WIDTH)], mine.at[slot])
            )
        right_own = local(right_root.at[own_rows, :], right_cols.at[own_rows, :])
        left_own = local(left_root.at[own_rows, :], left_full.at[own_rows, own_cols])
        m_in = local(adam_m, m_buf)
        v_in = local(adam_v, v_buf)
        w_in = local(weights, w_buf)
        ls_in = local(left_stat, ls_buf)
        rs_in = local(right_stat, rs_buf)
        pl.semaphore_wait(barrier, OWNERS - 1 + GROUP - 1)

    with jax.named_scope("reduce"):
        pairs = []
        for slot, row in enumerate(order):
            pairs.append(
                remote(
                    parts.at[:, span((row * 2 + 1 - c) * WIDTH, WIDTH)], pre.at[slot], to_mate
                )
            )
        for pair in pairs:
            pair.start()
        left_move = Exchange(
            lambda p: left_root.at[span(p * ROWS, ROWS), :],
            lambda rows: left_full.at[rows, own_cols], ROWS,
        )
        right_move = Exchange(
            lambda p: right_root.at[span(p * ROWS, ROWS), :],
            lambda rows: right_cols.at[rows, :], ROWS,
        )
        left_move.start()
        right_move.start()

        lo, hi = pl.ds(0, HALF), pl.ds(HALF, HALF)
        chunk = 64

        def add_up(target, first, rows, terms):
            def one(i, carry):
                at = span(first + i * chunk, chunk)
                total = terms[0](at).astype(F32)
                for term in terms[1:]:
                    total = total + term(at).astype(F32)
                target[at, :] = total.astype(BF16)
                return carry

            lax.fori_loop(0, rows // chunk, one, 0)

        def both(slot):
            mine_in[slot].wait()
            pairs[slot].wait_recv()
            return (lambda at: mine[slot, at, :], lambda at: pre[slot, at, :])

        far_up = remote(ps.at[0, lo, :], rel_a, to_up)
        far_down = remote(ps.at[0, hi, :], rel_b, to_down)
        up_hi = remote(ps.at[1, hi, :], from_minus.at[hi, :], to_up)
        down_lo = remote(ps.at[2, lo, :], from_plus.at[lo, :], to_down)
        up_lo = remote(ps.at[1, lo, :], from_minus.at[lo, :], to_up)
        down_hi = remote(ps.at[2, hi, :], from_plus.at[hi, :], to_down)

        terms = both(0)
        add_up(ps.at[0], 0, B, terms)
        far_up.start()
        far_down.start()
        terms = both(1)
        add_up(ps.at[1], HALF, HALF, terms)
        up_hi.start()
        terms_down = both(2)
        add_up(ps.at[2], 0, HALF, terms_down)
        down_lo.start()
        far_up.wait_recv()
        add_up(ps.at[1], 0, HALF, terms + (lambda at: rel_a[at, :],))
        up_lo.start()
        far_down.wait_recv()
        add_up(
            ps.at[2], HALF, HALF,
            terms_down + (lambda at: rel_b[span(at.start - HALF, chunk), :],),
        )
        down_hi.start()

        left_move.wait_recv()
        left_own.wait()
        left_gather = Gather(left_full)
        left_gather.start()

        terms = both(3)
        for copy in (up_hi, down_lo, up_lo, down_hi):
            copy.wait_recv()
        add_up(
            grad, 0, B, terms + (lambda at: from_minus[at, :], lambda at: from_plus[at, :])
        )

    with jax.named_scope("spread"):
        grad_move = Exchange(
            lambda p: grad.at[span(p * ROWS, ROWS), :], lambda rows: grad_cols.at[rows, :], ROWS
        )
        grad_move.start()
        grad_cols[own_rows, :] = grad[own_rows, :]

        def to_blocks(b, carry):
            by_block[b] = grad[span(b * ROWS, ROWS), :]
            return carry

        lax.fori_loop(0, OWNERS, to_blocks, 0)
        by_block[NONE] = jnp.zeros((ROWS, WIDTH), BF16)
        slot_moves = []
        for k in range(CAP):

            def pack(o, carry, k=k):
                q = o * CAP + k
                packed[k, span(o * ROWS, ROWS), :] = by_block[ids_ref[q]]
                return carry

            lax.fori_loop(0, OWNERS, pack, 0)
            move = Exchange(
                lambda p, k=k: packed.at[k, span(p * ROWS, ROWS), :],
                lambda rows, k=k: slots.at[k, rows, own_cols], ROWS,
            )
            move.start()
            slots[k, own_rows, own_cols] = packed[k, own_rows, :]
            slot_moves.append(move)

    left_gather.relay_one()
    with jax.named_scope("moments"):
        m_in.wait()
        v_in.wait()

        def adam(b, carry):
            at = span(b * ROWS, ROWS)
            m_new, v_new, direction = adam_direction(
                grad[at, :].astype(F32), m_buf[at, :], v_buf[at, :]
            )
            m_buf[at, :] = m_new
            v_buf[at, :] = v_new
            sums[pl.ds(b, 1), :] = jnp.sum(direction * direction, axis=0, keepdims=True)
            return carry

        lax.fori_loop(0, OWNERS, adam, 0)
    left_gather.relay_two()
    left_gather.relay_three()
    left_gather.finish()

    def product(target, lhs, rhs):
        def one(i, carry):
            at = span(i * 256, 256)
            target(
                at, jnp.dot(lhs[at, :], rhs, preferred_element_type=F32)
            )
            return carry

        lax.fori_loop(0, B // 256, one, 0)

    with jax.named_scope("mixed"):
        grad_move.wait_recv()

        def keep_mixed(at, value):
            mixed_full[at, own_cols] = value.astype(BF16)

        product(keep_mixed, left_full, grad_cols[...])
        mixed_gather = Gather(mixed_full)
        mixed_gather.start()
        mixed_gather.relay_one()
    slot_gathers = [Gather(slots.at[k]) for k in range(CAP)]
    slot_moves[0].wait_recv()
    slot_gathers[0].start()
    mixed_gather.relay_two()
    mixed_gather.relay_three()
    slot_gathers[0].relay_one()
    mixed_gather.finish()

    with jax.named_scope("precond"):
        right_move.wait_recv()
        right_own.wait()
        tile_one[...] = jnp.zeros_like(tile_one)
        rhs_right = right_cols[...]

        def one(i, total):
            at = span(i * 256, 256)
            value = jnp.dot(mixed_full[at, :], rhs_right, preferred_element_type=F32)
            pre_half[at, :] = value.astype(BF16)
            return total + jnp.sum(value * value, axis=0, keepdims=True)

        square = lax.fori_loop(0, B // 256, one, jnp.zeros((1, WIDTH), F32))
        norm = jnp.sum(square, axis=1, keepdims=True)
        lane = lax.broadcasted_iota(jnp.int32, (8, 128), 1)
        line = lax.broadcasted_iota(jnp.int32, (8, 128), 0)
        block_sums = jnp.sum(sums[...], axis=1, keepdims=True)
        rows_id = lax.broadcasted_iota(jnp.int32, (OWNERS, 128), 0)
        lanes_id = lax.broadcasted_iota(jnp.int32, (OWNERS, 128), 1)
        adam_row = jnp.sum(jnp.where(rows_id == lanes_id, block_sums, 0.0), axis=0, keepdims=True)
        shampoo_tile = jnp.where((line == 0) & (lane == s), norm, 0.0)
        tile = jnp.where(line == 1, adam_row, shampoo_tile)
        tile_one[...] = tile
        norm_one[span(s * 8, 8), :] = tile
        norm_move = Exchange(lambda p: tile_one, lambda rows: norm_one.at[rows, :], 8)
        norm_move.start()
        back_move = Exchange(
            lambda p: pre_half.at[span(p * ROWS, ROWS), :],
            lambda rows: pre_tile.at[rows, :], ROWS,
        )
        back_move.start()
        pre_tile[own_rows, :] = pre_half[own_rows, :]

    ls_in.wait()
    rs_in.wait()

    def grams(k):
        with jax.named_scope("grams"):
            row_block = slots[k, own_cols, :]

            def left(i, carry):
                at = span(i * 256, 256)
                gram = lax.dot_general(
                    slots[k, at, :], row_block, (((1,), (1,)), ((), ())),
                    preferred_element_type=F32,
                )
                ls_buf[k, at, :] = BETA_STAT * ls_buf[k, at, :] + (1.0 - BETA_STAT) * gram
                return carry

            lax.fori_loop(0, B // 256, left, 0)
            flipped = slots[k, :, own_cols].T

            def right(i, carry):
                at = span(i * 256, 256)
                gram = jnp.dot(flipped, slots[k, :, at], preferred_element_type=F32).T
                rs_buf[k, at, :] = BETA_STAT * rs_buf[k, at, :] + (1.0 - BETA_STAT) * gram
                return carry

            lax.fori_loop(0, B // 256, right, 0)

    slot_gathers[0].relay_two()
    slot_moves[1].wait_recv()
    slot_gathers[1].start()
    slot_gathers[0].relay_three()

    with jax.named_scope("norms"):
        norm_move.wait_recv()
        half_sum = jnp.sum(norm_one[...].reshape(OWNERS, 8, 128), axis=0)
        tile_two[...] = half_sum
        norm_two[span(j * 8, 8), :] = half_sum
        send, recv = new_sem()

        def share(q, carry):
            other = lax.rem(j + q, GROUP)
            pltpu.make_async_remote_copy(
                src_ref=tile_two, dst_ref=norm_two.at[span(j * 8, 8), :], send_sem=send,
                recv_sem=recv,
                device_id={"tensor": other // 2, "section": lax.rem(other, 2)},
                device_id_type=MESH,
            ).start()
            return carry

        lax.fori_loop(1, GROUP, share, 0)
        seven = norm_two.at[pl.ds(0, (GROUP - 1) * 8), :]
        shared = Copy(seven, seven, send, recv, to_mate)
        sent.append(shared)

    slot_gathers[1].relay_one()
    slot_gathers[0].finish()
    grams(0)
    slot_gathers[1].relay_two()
    slot_moves[2].wait_recv()
    slot_gathers[2].start()
    slot_gathers[1].relay_three()

    with jax.named_scope("update"):
        shared.wait_recv()
        totals = jnp.sum(norm_two[...].reshape(GROUP, 8, 128), axis=0)
        names_down = jnp.zeros((OWNERS, 128), jnp.int32)
        names_along = jnp.full((OWNERS, 128), -1, jnp.int32)
        for b in range(OWNERS):
            names_down = jnp.where(rows_id == b, matrix_ref[b], names_down)
            names_along = jnp.where(lanes_id == b, matrix_ref[b], names_along)
        same_value = (names_down == names_along).astype(F32)
        shampoo = jnp.sum(same_value * totals[0:1, :], axis=1, keepdims=True)
        adam_sum = jnp.sum(same_value * totals[1:2, :], axis=1, keepdims=True)
        counts = jnp.sum(same_value, axis=1, keepdims=True) * float(B * B)
        scale = jnp.sqrt(adam_sum / (shampoo + FLOOR_RATE * counts))
        scales[...] = jnp.broadcast_to(scale, (OWNERS, 128))
        back_move.wait_recv()
        w_in.wait()

        def update(b, carry):
            at = span(b * ROWS, ROWS)
            value = w_buf[at, :].astype(F32)
            step = scales[pl.ds(b, 1), :] * pre_tile[at, :].astype(F32)
            new_full[at, own_cols] = (value - LEARNING * (step + DECAY_RATE * value)).astype(BF16)
            return carry

        lax.fori_loop(0, OWNERS, update, 0)
        new_gather = Gather(new_full)
        new_gather.start()
    slot_gathers[1].finish()
    slot_gathers[2].relay_one()
    grams(1)
    new_gather.relay_one()
    slot_gathers[2].relay_two()
    slot_gathers[2].relay_three()
    new_gather.relay_two()
    new_gather.relay_three()
    slot_gathers[2].finish()
    grams(2)
    new_gather.finish()

    for copy in sent:
        copy.wait_send()


def fused_step(ids, matrix, parts, weights, m, v, left_stat, right_stat, left_root, right_root):
    hbm = pl.BlockSpec(memory_space=pltpu.HBM)
    vmem = pl.BlockSpec(memory_space=pltpu.VMEM)
    smem = pl.BlockSpec(memory_space=pltpu.SMEM)
    slab = (B, WIDTH)
    full = (B, B)
    shapes = (
        jax.ShapeDtypeStruct(full, BF16),
        jax.ShapeDtypeStruct(slab, F32),
        jax.ShapeDtypeStruct(slab, F32),
        jax.ShapeDtypeStruct((CAP,) + slab, F32),
        jax.ShapeDtypeStruct((CAP,) + slab, F32),
    )
    stay = [
        pltpu.with_memory_space_constraint(x, pltpu.HBM)
        for x in (parts, weights, m, v, left_stat, right_stat, left_root, right_root)
    ]
    results = pl.pallas_call(
        kernel,
        out_shape=tuple(pltpu.VMEM(x.shape, x.dtype) for x in shapes),
        in_specs=[smem] * 2 + [hbm] * 8,
        out_specs=(vmem,) * 5,
        scratch_shapes=[
            pltpu.VMEM((RING,) + slab, BF16),
            pltpu.VMEM((RING,) + slab, BF16),
            pltpu.VMEM((3,) + slab, BF16),
            pltpu.VMEM((HALF, WIDTH), BF16),
            pltpu.VMEM((HALF, WIDTH), BF16),
            pltpu.VMEM(slab, BF16),
            pltpu.VMEM(slab, BF16),
            pltpu.VMEM(slab, BF16),
            pltpu.VMEM((OWNERS + 1, ROWS, WIDTH), BF16),
            pltpu.VMEM((CAP,) + slab, BF16),
            pltpu.VMEM(full, BF16),
            pltpu.VMEM(full, BF16),
            pltpu.VMEM((CAP,) + full, BF16),
            pltpu.VMEM(slab, BF16),
            pltpu.VMEM(slab, BF16),
            pltpu.VMEM(slab, BF16),
            pltpu.VMEM(slab, BF16),
            pltpu.VMEM(slab, BF16),
            pltpu.VMEM((8, 128), F32),
            pltpu.VMEM((OWNERS * 8, 128), F32),
            pltpu.VMEM((8, 128), F32),
            pltpu.VMEM((GROUP * 8, 128), F32),
            pltpu.VMEM((OWNERS, 128), F32),
            pltpu.VMEM((OWNERS, 128), F32),
            pltpu.SemaphoreType.DMA((96,)),
            pltpu.SemaphoreType.DMA((96,)),
            pltpu.SemaphoreType.DMA((32,)),
        ],
        compiler_params=pltpu.CompilerParams(
            collective_id=0, has_side_effects=True, vmem_limit_bytes=VMEM_LIMIT
        ),
        name="shampoo_step",
    )(ids, matrix, *stay)
    return pl.pallas_call(
        write_out,
        out_shape=shapes,
        in_specs=[vmem] * 5,
        out_specs=(hbm,) * 5,
        scratch_shapes=[pltpu.SemaphoreType.DMA((5,))],
        compiler_params=pltpu.CompilerParams(vmem_limit_bytes=WRITE_LIMIT),
        name="write_out",
    )(*results)


def write_out(*refs):
    copies = [
        pltpu.make_async_copy(src, dst, refs[10].at[i])
        for i, (src, dst) in enumerate(zip(refs[:5], refs[5:10]))
    ]
    for copy in copies:
        copy.start()
    for copy in copies:
        copy.wait()


def shards(
    grad_parts,
    weights,
    adam_m,
    adam_v,
    left_stat,
    right_stat,
    left_root,
    right_root,
    block_owner,
    block_matrix,
    factors,
    factor_grad,
    factor_m,
    factor_v,
):
    block_ids = slot_blocks(block_owner)
    new_weights, adam_m_new, adam_v_new, left_new, right_new = fused_step(
        block_ids,
        block_matrix,
        grad_parts.reshape(B, B),
        weights.reshape(B, WIDTH),
        adam_m.reshape(B, WIDTH),
        adam_v.reshape(B, WIDTH),
        left_stat,
        right_stat,
        left_root.reshape(B, WIDTH),
        right_root.reshape(B, WIDTH),
    )
    factor_m_new, factor_v_new, factor_step = adam_direction(
        factor_grad.astype(F32), factor_m, factor_v
    )
    factors_new = factors - LEARNING * (factor_step + DECAY_RATE * factors)
    return (
        new_weights.reshape(OWNERS, ROWS, B),
        adam_m_new.reshape(OWNERS, ROWS, WIDTH),
        adam_v_new.reshape(OWNERS, ROWS, WIDTH),
        left_new,
        right_new,
        factors_new,
        factor_m_new,
        factor_v_new,
    )


def solution(mesh):
    row = ("tensor", "section")
    slab = P(None, "shard", row)
    stat = P("shard", None, row)
    factor = P("shard", row)
    in_specs = (
        P(row, None, "shard", None), slab, slab, slab, stat, stat, slab, slab, P(), P(),
        factor, factor, factor, factor,
    )
    out_specs = (P(None, "shard", None), slab, slab, stat, stat, factor, factor, factor)
    return jax.shard_map(shards, mesh=mesh, in_specs=in_specs, out_specs=out_specs, check_vma=False)
```
